32 devices in a mesh: grp: 2 (over y), seq: 8 (over z, x), mdl: 2 (over core).
Axes of the slice: x: 2, y: 2, z: 4, core: 2. Of those that a mesh axis runs over, the one named last changes fastest.
Arguments:
- tokens_in: bfloat16 [64, 8192], P(('grp', 'seq'), 'mdl'), parts along dimension 0, may hold values from -180 to 180
- norm_gain: float32 [8192], P('mdl'), may hold values from 0.5 to 1.5
- in_proj: bfloat16 [8, 3, 1024, 8192], P('seq', None, None, 'mdl'), may hold values from -0.0625 to 0.0625
- short_taps: float32 [7, 3, 8192], P(None, None, 'seq'), may hold values from -2.5 to 2.5
- long_taps: float32 [512, 128], replicated, may hold values from -0.5 to 0.5
- skip_bias: float32 [8192], P('seq'), may hold values from -6 to 6
- out_proj: bfloat16 [8192, 2, 4096], P('seq', 'mdl'), may hold values from -0.0625 to 0.0625
Outputs:
- mixed: bfloat16 [64, 8192], P('grp', 'seq'), parts along dimension 0
The draws below stay inside these ranges and needn't reach their ends.
There are 2 independent parts, one for each index of `grp`. The reference program is written for one: setup_inputs(seed, part) draws one part's arguments, and reference() takes and returns one part's arrays. A program takes and returns all parts, laid end to end along the dimension named above; an argument that names none is the same for every part. Nothing has to cross between parts.
All inputs are finite; a program needn't handle non-finite values.
Results may differ from the reference program's by a relative error of at most 0.007.
Values may be sent and summed in bfloat16 or wider, within the bound.
A program may use at most 320 MiB of HBM per device.

```python
import math
import jax
import jax.numpy as jnp
from jax import lax

D = 8192
GROUP_CH = 16
FL = 128
SK = 7
TOKENS = 32
CH = 512
HALF = 4096
GROUPS = 512
N_SEQ = 8


def draw_tokens_in(key, part):
    key_base = jax.random.fold_in(key, 11)
    key_one, key_two, key_three = jax.random.split(key_base, 3)
    col_scale = jnp.exp(jax.random.uniform(key_three, (D,), jnp.float32, math.log(0.3), math.log(3.0)))
    base_vals = jnp.clip(jax.random.normal(key_one, (TOKENS, D), jnp.float32), -6.0, 6.0)
    row_scale = jnp.exp(jax.random.uniform(key_two, (TOKENS,), jnp.float32, 0.0, math.log(10.0)))
    return (base_vals * row_scale[:, None] * col_scale[None, :]).astype(jnp.bfloat16)


def level_of(own_key, dims, pieces, least, largest):
    def one(axis_at, parts):
        draws = jax.random.uniform(jax.random.fold_in(jax.random.fold_in(own_key, 6), axis_at), (parts,), jnp.float32, least / len(pieces), largest / len(pieces))
        return jnp.repeat(jnp.exp(draws), dims[axis_at] // parts).reshape((-1,) + (1,) * (len(dims) - axis_at - 1))

    gain = one(*pieces[0])
    for cut in pieces[1:]:
        gain = gain * one(*cut)
    return gain


def scatter_about(rng, shape, scale, reach, cuts=(), held_as=jnp.bfloat16):
    level = level_of(rng, shape, cuts, -0.22, 0.18) if cuts else 1.0
    entries = jax.random.normal(rng, shape, jnp.float32) * scale * level
    return jnp.minimum(jnp.maximum(entries, -reach), reach).astype(held_as)


def setup_inputs(seed: int = 0, part: int = 0) -> dict:
    seeds = jax.random.split(jax.random.key(seed), 8)
    part_keys = jax.random.split(jax.random.fold_in(seeds[7], part), 8)
    tokens_in = draw_tokens_in(jax.random.fold_in(jax.random.fold_in(seeds[7], part), 71), part)
    norm_gain = jnp.clip(1.0 + 0.1 * jax.random.normal(seeds[1], (D,), jnp.float32), 0.5, 1.5)
    in_proj = scatter_about(seeds[2], (N_SEQ, 3, 2 * CH, D), D ** -0.5, 0.0625, ((0, 8), (3, 2)))
    short_taps = scatter_about(seeds[3], (SK, 3, D), 0.4, 2.5, ((2, 8),), jnp.float32)
    long_taps = scatter_about(seeds[4], (GROUPS, FL), 0.09, 0.5, (), jnp.float32)
    skip_bias = scatter_about(seeds[5], (D,), 1.0, 6.0, ((0, 8),), jnp.float32)
    out_proj = scatter_about(seeds[6], (D, 2, HALF), D ** -0.5, 0.0625, ((0, 8), (1, 2)))
    return dict(tokens_in=tokens_in, norm_gain=norm_gain, in_proj=in_proj, short_taps=short_taps, long_taps=long_taps, skip_bias=skip_bias, out_proj=out_proj)


EPSILON = 1e-06

def reference(tokens_in, norm_gain, in_proj, short_taps, long_taps, skip_bias, out_proj):
    values = tokens_in.astype(jnp.float32)
    mean_square = lax.optimization_barrier(jnp.mean(values * values, axis=1, keepdims=True))
    normed = (values * lax.rsqrt(mean_square + EPSILON) * norm_gain[None, :]).astype(jnp.bfloat16)
    weights_in = jnp.transpose(in_proj, (3, 1, 0, 2)).reshape(D, 3 * D)
    projected = jnp.dot(normed, weights_in, preferred_element_type=jnp.float32).reshape(TOKENS, 3, D)
    padded = jnp.pad(projected, ((SK - 1, 0), (0, 0), (0, 0)))
    features = jnp.zeros((TOKENS, 3, D), jnp.float32)
    for offset in range(SK):
        features = features + short_taps[offset][None, :, :] * padded[SK - 1 - offset:SK - 1 - offset + TOKENS]
    gated_prod = features[:, 1, :] * features[:, 2, :]
    channel_taps = jnp.repeat(long_taps, GROUP_CH, axis=0)
    mixed_long = skip_bias[None, :] * gated_prod
    shifted = jnp.pad(gated_prod, ((FL - 1, 0), (0, 0)))
    for offset in range(FL):
        mixed_long = mixed_long + channel_taps[:, offset][None, :] * shifted[FL - 1 - offset:FL - 1 - offset + TOKENS]
    gated_out = (features[:, 0, :] * mixed_long).astype(jnp.bfloat16)
    weights_out = jnp.transpose(out_proj.reshape(D, 2, N_SEQ, CH), (2, 1, 3, 0)).reshape(D, D)
    return jnp.dot(gated_out, weights_out, preferred_element_type=jnp.float32).astype(jnp.bfloat16)
```

```python
import functools

import jax
import jax.numpy as jnp
from jax import lax
from jax.experimental import pallas as pl
from jax.experimental.pallas import tpu as pltpu
from jax.sharding import PartitionSpec as P

D = 8192


EPSILON = 1e-06

N_Z = 4


def build_toeplitz(channel_taps):
    chan_width, filt_len = channel_taps.shape
    blank = jnp.zeros((chan_width, filt_len), jnp.float32)
    framed = jnp.concatenate([blank, channel_taps, blank], axis=1)
    flipped = framed[:, ::-1]
    repeated = jnp.tile(flipped, (1, filt_len + 1))
    window = repeated[:, filt_len - 1 : filt_len - 1 + filt_len * (3 * filt_len - 1)]
    return window.reshape(chan_width, filt_len, 3 * filt_len - 1)[:, :, : 2 * filt_len]


def mix_channels(summed, short_local, bias_local, long_taps, first_channel, chan_width):
    token_count = summed.shape[0]
    taps_short = short_local.shape[0]
    padded = jnp.pad(summed, ((taps_short - 1, 0), (0, 0), (0, 0)))
    features = jnp.zeros(summed.shape, jnp.float32)
    for offset in range(taps_short):
        features = (
            features
            + short_local[offset][None, :, :]
            * padded[taps_short - 1 - offset : taps_short - 1 - offset + token_count]
        )
    gated_prod = features[:, 1, :] * features[:, 2, :]
    group_count = long_taps.shape[0]
    filt_len = long_taps.shape[1]
    group_width = D // group_count
    channel_ids = first_channel + jnp.arange(chan_width, dtype=jnp.int32)
    select_groups = (
        channel_ids[:, None] // group_width == jnp.arange(group_count, dtype=jnp.int32)[None, :]
    ).astype(jnp.float32)
    channel_taps = jnp.dot(select_groups, long_taps, precision=lax.Precision.HIGHEST)
    toeplitz = build_toeplitz(channel_taps)
    blocks = -(-token_count // filt_len)
    framed = jnp.pad(gated_prod, ((filt_len, blocks * filt_len - token_count), (0, 0))).reshape(
        blocks + 1, filt_len, chan_width
    )
    block_pairs = jnp.concatenate([framed[:-1], framed[1:]], axis=1)
    mixed_long = jnp.einsum("ctk,nkc->ntc", toeplitz, block_pairs, precision=lax.Precision.HIGHEST)
    mixed_long = mixed_long.reshape(blocks * filt_len, chan_width)[:token_count]
    mixed_long = mixed_long + bias_local[None, :] * gated_prod
    return (features[:, 0, :] * mixed_long).astype(jnp.bfloat16)


def contract_last(left, right):
    return lax.dot_general(
        left, right, (((1,), (1,)), ((), ())), preferred_element_type=jnp.float32
    )


def per_device(tokens_in, norm_gain, in_proj, short_taps, long_taps, skip_bias, out_proj):
    half_width = tokens_in.shape[1]
    chan_dev = in_proj.shape[2] // 2
    seq_index = lax.axis_index("seq")
    mdl_index = lax.axis_index("mdl")
    weights_in = in_proj.reshape(-1, half_width)
    values = tokens_in.astype(jnp.float32)
    squares = lax.psum(jnp.sum(values * values, axis=1), "mdl")
    scale_rows = lax.rsqrt(squares / D + EPSILON)
    normed = (values * scale_rows[:, None] * norm_gain[None, :]).astype(jnp.bfloat16)
    partial_value = contract_last(lax.all_gather(normed, "seq", axis=0, tiled=True), weights_in)
    token_count = partial_value.shape[0]
    partial_value = partial_value.reshape(token_count, 3, 2, chan_dev)
    summed = lax.psum_scatter(partial_value, "mdl", scatter_dimension=2, tiled=True).reshape(
        token_count, 3, chan_dev
    )
    short_local = lax.dynamic_slice_in_dim(short_taps, mdl_index * chan_dev, chan_dev, 2)
    bias_local = lax.dynamic_slice_in_dim(skip_bias, mdl_index * chan_dev, chan_dev, 0)
    own_mixed = mix_channels(
        summed,
        short_local,
        bias_local,
        long_taps,
        seq_index * 2 * chan_dev + mdl_index * chan_dev,
        chan_dev,
    )
    out_cols = out_proj.shape[0]
    out_rows = out_proj.reshape(out_cols, -1)
    folded = contract_last(lax.all_gather(own_mixed, "seq", axis=1, tiled=True), out_rows)
    return lax.psum(folded, "mdl").astype(jnp.bfloat16)


def mixer_kernel(
    tok, gain, w_in, staps, ltaps, bias, w_out, out,
    wbuf, wobuf, xg, xf, xb, gainv, stv, ltv, biasv,
    sq_own, sq_part, sq_recv, scales, p_send, p_recv, p_own, padded, gp, tex, gg, facc, frecv,
    w_sems, wo_sems, small_sems, swap_sems, sq_send, sq_get, p_send_sems, p_recv_sems,
    g1_send, g1_recv, g2_send, g2_recv, f_sems,
):
    n_seq, t_loc, half = xg.shape
    tokens = n_seq * t_loc
    chan = p_own.shape[2]
    short_len = stv.shape[1]
    used_taps = tex.shape[0]
    s = lax.axis_index("seq")
    m = lax.axis_index("mdl")
    mesh_ids = pl.DeviceIdType.MESH
    partner = {"mdl": 1 - m}
    first = lax.rem(s, 2)

    shifts = tuple(
        (step, cross)
        for step in (0, 1, N_Z - 1) + tuple(range(2, N_Z - 1))
        for cross in (0, 1)
        if step or cross
    )

    def peer(shift):
        step, cross = shift
        flip = cross * (1 - 2 * first)
        return lax.rem(s + 2 * step, n_seq) + flip

    def source(shift):
        step, cross = shift
        flip = cross * (1 - 2 * first)
        return lax.rem(s + n_seq - 2 * step, n_seq) + flip

    barrier = pltpu.get_barrier_semaphore()
    for shift in shifts:
        pl.semaphore_signal(
            barrier, inc=1, device_id={"seq": peer(shift)}, device_id_type=mesh_ids
        )
    pl.semaphore_signal(barrier, inc=1, device_id=partner, device_id_type=mesh_ids)

    own_tok = pltpu.make_async_copy(tok, xg.at[s], small_sems.at[0])
    own_tok.start()

    def w_copy(c):
        branch = lax.rem(c, 3)
        side = jnp.where(c < 3, 1 - m, m)
        row = pl.multiple_of(branch * (2 * chan) + side * chan, chan)
        return pltpu.make_async_copy(w_in.at[pl.ds(row, chan), :], wbuf.at[c], w_sems.at[c])

    def wo_copy(a):
        return pltpu.make_async_copy(
            w_out.at[:, pl.ds(a * chan, chan)], wobuf.at[a], wo_sems.at[a]
        )

    col = pl.multiple_of(m * chan, chan)
    groups = ltv.shape[0]
    first_group = pl.multiple_of((s * 2 + m) * groups, groups)
    small = [
        pltpu.make_async_copy(gain, gainv, small_sems.at[1]),
        pltpu.make_async_copy(staps.at[:, :, pl.ds(col, chan)], stv, small_sems.at[2]),
        pltpu.make_async_copy(ltaps.at[pl.ds(first_group, groups), :], ltv, small_sems.at[3]),
        pltpu.make_async_copy(bias.at[:, pl.ds(col, chan)], biasv, small_sems.at[4]),
    ]
    for copy in small:
        copy.start()
    for c in range(6):
        w_copy(jnp.int32(c)).start()

    def lane_sums(values):
        total = None
        for k in range(half // 128):
            piece = values[:, k * 128 : (k + 1) * 128]
            total = piece * piece if total is None else total + piece * piece
        return total

    own_tok.wait()
    sq_own[...] = lane_sums(xg[s].astype(jnp.float32))
    pl.semaphore_wait(barrier, n_seq)

    def gather_copies(buf, send, recv):
        return [
            pltpu.make_async_remote_copy(
                src_ref=buf.at[s], dst_ref=buf.at[s],
                send_sem=send.at[k], recv_sem=recv.at[k],
                device_id={"seq": peer(shift)}, device_id_type=mesh_ids,
            )
            for k, shift in enumerate(shifts)
        ]

    swap = pltpu.make_async_remote_copy(
        src_ref=sq_own, dst_ref=sq_part,
        send_sem=swap_sems.at[0], recv_sem=swap_sems.at[1],
        device_id=partner, device_id_type=mesh_ids,
    )
    swap.start()
    gather = gather_copies(xg, g1_send, g1_recv)
    for copy in gather:
        copy.start()
    swap.wait()
    sq_recv[s] = sq_own[...] + sq_part[...]
    sums = gather_copies(sq_recv, sq_send, sq_get)
    for copy in sums:
        copy.start()

    for copy in small:
        copy.wait()
    taps = jnp.transpose(ltv[...])[:used_taps, :]
    rows = lax.broadcasted_iota(jnp.int32, (groups, chan), 0)
    cols = lax.broadcasted_iota(jnp.int32, (groups, chan), 1)
    width = chan // groups
    pick = jnp.where(
        (cols >= rows * width) & (cols < rows * width + width), 1.0, 0.0
    ).astype(jnp.bfloat16)
    high = taps.astype(jnp.bfloat16)
    rest = taps - high.astype(jnp.float32)
    mid = rest.astype(jnp.bfloat16)
    low = (rest - mid.astype(jnp.float32)).astype(jnp.bfloat16)
    tex[...] = (
        jnp.dot(high, pick, preferred_element_type=jnp.float32)
        + jnp.dot(mid, pick, preferred_element_type=jnp.float32)
    ) + jnp.dot(low, pick, preferred_element_type=jnp.float32)
    padded[:, :8, :] = jnp.zeros((3, 8, chan), jnp.float32)
    gp[:tokens, :] = jnp.zeros((tokens, chan), jnp.float32)

    for copy in gather:
        copy.wait_recv()
    for a in range(n_seq):
        xf[a * t_loc : (a + 1) * t_loc, :] = xg[a].astype(jnp.float32)
    for copy in sums:
        copy.wait_recv()
    for a in range(n_seq):
        scales[a * t_loc : (a + 1) * t_loc, :] = sq_recv[a]
    squares = jnp.sum(scales[...], axis=1, keepdims=True)
    scale_rows = lax.rsqrt(squares / D + EPSILON)
    xb[...] = (xf[...] * scale_rows * gainv[...]).astype(jnp.bfloat16)

    def p_copy(c):
        return pltpu.make_async_remote_copy(
            src_ref=p_send.at[c], dst_ref=p_recv.at[c],
            send_sem=p_send_sems.at[c], recv_sem=p_recv_sems.at[c],
            device_id=partner, device_id_type=mesh_ids,
        )

    for a in range(n_seq):
        wo_copy(a).start()

    @pl.loop(0, 3)
    def _(c):
        w_copy(c).wait()
        p_send[c] = jnp.transpose(contract_last(wbuf[c], xb[...]))
        p_copy(c).start()

    @pl.loop(0, 3)
    def _(c):
        w_copy(c + 3).wait()
        p_own[c] = jnp.transpose(contract_last(wbuf[c + 3], xb[...]))

    features = []
    for c in range(3):
        p_copy(c).wait()
        padded[c, 8 : 8 + tokens, :] = p_own[c] + p_recv[c]
        value = None
        for i in range(short_len):
            term = stv[c, i : i + 1, :] * padded[c, 8 - i : 8 - i + tokens, :]
            value = term if value is None else value + term
        features.append(value)
    gated = features[1] * features[2]
    gp[tokens : 2 * tokens, :] = gated
    mixed = biasv[...] * gated
    for i in range(used_taps):
        mixed = mixed + tex[i : i + 1, :] * gp[tokens - i : 2 * tokens - i, :]
    gg[s] = (features[0] * mixed).astype(jnp.bfloat16)

    gather2 = gather_copies(gg, g2_send, g2_recv)
    for copy in gather2:
        copy.start()
    for a in range(n_seq):
        wo_copy(a).wait()
    facc[...] = contract_last(gg[s], wobuf[s])
    for copy, shift in zip(gather2, shifts):
        copy.wait_recv()
        slot = source(shift)
        facc[...] += contract_last(gg[slot], wobuf[slot])

    final = pltpu.make_async_remote_copy(
        src_ref=facc, dst_ref=frecv, send_sem=f_sems.at[0], recv_sem=f_sems.at[1],
        device_id=partner, device_id_type=mesh_ids,
    )
    final.start()
    for copy in gather + sums + gather2:
        copy.wait_send()
    final.wait()
    out[...] = (facc[...] + frecv[...]).astype(out.dtype)


def fused_device(tokens_in, norm_gain, in_proj, short_taps, long_taps, skip_bias, out_proj):
    n_seq = lax.axis_size("seq")
    t_loc, half = tokens_in.shape
    tokens = n_seq * t_loc
    chan = in_proj.shape[2] // 2
    cols = out_proj.shape[0]
    group_count, filt_len = long_taps.shape
    groups = chan * group_count // D
    used_taps = min(filt_len, tokens)
    f32, bf16 = jnp.float32, jnp.bfloat16
    vmem, dma = pltpu.VMEM, pltpu.SemaphoreType.DMA
    anywhere = pl.BlockSpec(memory_space=pl.ANY)
    return pl.pallas_call(
        mixer_kernel,
        name="mixer",
        out_shape=vmem((tokens, cols), bf16),
        in_specs=[anywhere] * 7,
        out_specs=pl.BlockSpec(memory_space=pltpu.VMEM),
        scratch_shapes=[
            vmem((6, chan, half), bf16),
            vmem((n_seq, cols, chan), bf16),
            vmem((n_seq, t_loc, half), bf16),
            vmem((tokens, half), f32),
            vmem((tokens, half), bf16),
            vmem((1, half), f32),
            vmem((3, short_taps.shape[0], chan), f32),
            vmem((groups, filt_len), f32),
            vmem((1, chan), f32),
            vmem((t_loc, 128), f32),
            vmem((t_loc, 128), f32),
            vmem((n_seq, t_loc, 128), f32),
            vmem((tokens, 128), f32),
            vmem((3, tokens, chan), f32),
            vmem((3, tokens, chan), f32),
            vmem((3, tokens, chan), f32),
            vmem((3, 8 + tokens, chan), f32),
            vmem((2 * tokens, chan), f32),
            vmem((used_taps, chan), f32),
            vmem((n_seq, tokens, chan), bf16),
            vmem((tokens, cols), f32),
            vmem((tokens, cols), f32),
            dma((6,)),
            dma((n_seq,)),
            dma((5,)),
            dma((2,)),
            dma((n_seq,)),
            dma((n_seq,)),
            dma((3,)),
            dma((3,)),
            dma((n_seq - 1,)),
            dma((n_seq - 1,)),
            dma((n_seq - 1,)),
            dma((n_seq - 1,)),
            dma((2,)),
        ],
        compiler_params=pltpu.CompilerParams(
            collective_id=0, has_side_effects=True, vmem_limit_bytes=60 * 1024 * 1024
        ),
    )(
        tokens_in,
        norm_gain.reshape(1, half),
        in_proj.reshape(-1, half),
        jnp.transpose(short_taps, (1, 0, 2)),
        long_taps,
        skip_bias.reshape(1, -1),
        out_proj.reshape(cols, -1),
    )


def fits_kernel(mesh, tokens_in, norm_gain, in_proj, short_taps, long_taps, skip_bias, out_proj):
    n_seq = mesh.shape["seq"]
    tokens = tokens_in.shape[0] // mesh.shape["grp"]
    chan = in_proj.shape[2] // 2
    half = tokens_in.shape[1] // 2
    weight_bytes = 2 * (in_proj.size + out_proj.size) // (2 * n_seq)
    return (
        n_seq == 2 * N_Z
        and mesh.shape["mdl"] == 2
        and chan % 256 == 0
        and half % 256 == 0
        and tokens % 16 == 0
        and tokens <= min(64, long_taps.shape[1])
        and short_taps.shape[0] <= 8
        and long_taps.shape[1] == 128
        and (chan * long_taps.shape[0] // D) % 8 == 0
        and weight_bytes <= 40 * 1024 * 1024
    )


def solution(mesh):
    in_specs = (
        P(("grp", "seq"), "mdl"),
        P("mdl"),
        P("seq", None, None, "mdl"),
        P(None, None, "seq"),
        P(),
        P("seq"),
        P("seq", "mdl", None),
    )
    out_specs = P("grp", "seq")

    def run(*arrays):
        body = fused_device if fits_kernel(mesh, *arrays) else per_device
        return jax.shard_map(
            body, mesh=mesh, in_specs=in_specs, out_specs=out_specs, check_vma=False
        )(*arrays)

    return run
```

```python
import functools

import jax
import jax.numpy as jnp
from jax import lax
from jax.experimental import pallas as pl
from jax.experimental.pallas import tpu as pltpu
from jax.sharding import PartitionSpec as P

D = 8192


EPSILON = 1e-06

N_Z = 4

SHIFTS = ((2, 1), (2, 0), (1, 1), (3, 1), (1, 0), (3, 0), (0, 1))
N_K = 4
W_AHEAD = 2
PARTS = ((0, 256), (256, 256))
STEPS = (
    ('x', 0),
    ('m', 0, 0, (0, 1)),
    ('m', 1, 0, (0, 1)),
    ('x', 1),
    ('m', 0, 1, (0, 1)),
    ('m', 1, 1, (0, 1)),
    ('x', 2),
    ('m', 0, 2, (0, 1)),
    ('x', 3),
    ('m', 0, 3, (0, 1)),
    ('m', 1, 2, (0,)),
    ('s',),
    ('c', 0),
    ('m', 1, 3, (0,)),
    ('m', 1, 2, (1,)),
    ('m', 1, 3, (1,)),
    ('c', 1),
)
ORDER = tuple(
    (step[1], step[2], side) for step in STEPS if step[0] == "m" for side in step[3]
)


def build_toeplitz(channel_taps):
    chan_width, filt_len = channel_taps.shape
    blank = jnp.zeros((chan_width, filt_len), jnp.float32)
    framed = jnp.concatenate([blank, channel_taps, blank], axis=1)
    flipped = framed[:, ::-1]
    repeated = jnp.tile(flipped, (1, filt_len + 1))
    window = repeated[:, filt_len - 1 : filt_len - 1 + filt_len * (3 * filt_len - 1)]
    return window.reshape(chan_width, filt_len, 3 * filt_len - 1)[:, :, : 2 * filt_len]


def mix_channels(summed, short_local, bias_local, long_taps, first_channel, chan_width):
    token_count = summed.shape[0]
    taps_short = short_local.shape[0]
    padded = jnp.pad(summed, ((taps_short - 1, 0), (0, 0), (0, 0)))
    features = jnp.zeros(summed.shape, jnp.float32)
    for offset in range(taps_short):
        features = (
            features
            + short_local[offset][None, :, :]
            * padded[taps_short - 1 - offset : taps_short - 1 - offset + token_count]
        )
    gated_prod = features[:, 1, :] * features[:, 2, :]
    group_count = long_taps.shape[0]
    filt_len = long_taps.shape[1]
    group_width = D // group_count
    channel_ids = first_channel + jnp.arange(chan_width, dtype=jnp.int32)
    select_groups = (
        channel_ids[:, None] // group_width == jnp.arange(group_count, dtype=jnp.int32)[None, :]
    ).astype(jnp.float32)
    channel_taps = jnp.dot(select_groups, long_taps, precision=lax.Precision.HIGHEST)
    toeplitz = build_toeplitz(channel_taps)
    blocks = -(-token_count // filt_len)
    framed = jnp.pad(gated_prod, ((filt_len, blocks * filt_len - token_count), (0, 0))).reshape(
        blocks + 1, filt_len, chan_width
    )
    block_pairs = jnp.concatenate([framed[:-1], framed[1:]], axis=1)
    mixed_long = jnp.einsum("ctk,nkc->ntc", toeplitz, block_pairs, precision=lax.Precision.HIGHEST)
    mixed_long = mixed_long.reshape(blocks * filt_len, chan_width)[:token_count]
    mixed_long = mixed_long + bias_local[None, :] * gated_prod
    return (features[:, 0, :] * mixed_long).astype(jnp.bfloat16)


def contract_last(left, right):
    return lax.dot_general(
        left, right, (((1,), (1,)), ((), ())), preferred_element_type=jnp.float32
    )


def per_device(tokens_in, norm_gain, in_proj, short_taps, long_taps, skip_bias, out_proj):
    half_width = tokens_in.shape[1]
    chan_dev = in_proj.shape[2] // 2
    seq_index = lax.axis_index("seq")
    mdl_index = lax.axis_index("mdl")
    weights_in = in_proj.reshape(-1, half_width)
    values = tokens_in.astype(jnp.float32)
    squares = lax.psum(jnp.sum(values * values, axis=1), "mdl")
    scale_rows = lax.rsqrt(squares / D + EPSILON)
    normed = (values * scale_rows[:, None] * norm_gain[None, :]).astype(jnp.bfloat16)
    partial_value = contract_last(lax.all_gather(normed, "seq", axis=0, tiled=True), weights_in)
    token_count = partial_value.shape[0]
    partial_value = partial_value.reshape(token_count, 3, 2, chan_dev)
    summed = lax.psum_scatter(partial_value, "mdl", scatter_dimension=2, tiled=True).reshape(
        token_count, 3, chan_dev
    )
    short_local = lax.dynamic_slice_in_dim(short_taps, mdl_index * chan_dev, chan_dev, 2)
    bias_local = lax.dynamic_slice_in_dim(skip_bias, mdl_index * chan_dev, chan_dev, 0)
    own_mixed = mix_channels(
        summed,
        short_local,
        bias_local,
        long_taps,
        seq_index * 2 * chan_dev + mdl_index * chan_dev,
        chan_dev,
    )
    out_cols = out_proj.shape[0]
    out_rows = out_proj.reshape(out_cols, -1)
    folded = contract_last(lax.all_gather(own_mixed, "seq", axis=1, tiled=True), out_rows)
    return lax.psum(folded, "mdl").astype(jnp.bfloat16)


def mixer_kernel(
    parts, tok, gain, w_in, staps, ltaps, bias, w_out, out,
    w_parts, wobuf, tokv, xg, xf, xb, gainv, stv, ltv, biasv,
    sq_own, sq_part, sq_recv, scales, accs, p_sends, p_recvs, p_owns, padded, gp, tex, ggs, facc, frecv,
    w_sems, wo_sems, small_sems, swap_sems, sq_send, sq_get, p_send_sems, p_recv_sems,
    g1_send, g1_recv, g2_send, g2_recv, f_sems,
):
    n_k, n_seq, t_loc, k_width = xg.shape
    tokens = n_seq * t_loc
    chan = stv.shape[2]
    short_len = stv.shape[1]
    used_taps = tex.shape[0]
    s = lax.axis_index("seq")
    m = lax.axis_index("mdl")
    mesh_ids = pl.DeviceIdType.MESH
    partner = {"mdl": 1 - m}
    first = lax.rem(s, 2)

    shifts = tuple((step, cross) for step, cross in SHIFTS)

    def peer(shift):
        step, cross = shift
        flip = cross * (1 - 2 * first)
        return lax.rem(s + 2 * step, n_seq) + flip

    def source(shift):
        step, cross = shift
        flip = cross * (1 - 2 * first)
        return lax.rem(s + n_seq - 2 * step, n_seq) + flip

    barrier = pltpu.get_barrier_semaphore()
    for shift in shifts:
        pl.semaphore_signal(
            barrier, inc=1, device_id={"seq": peer(shift)}, device_id_type=mesh_ids
        )
    pl.semaphore_signal(barrier, inc=1, device_id=partner, device_id_type=mesh_ids)

    own_tok = pltpu.make_async_copy(tok, tokv, small_sems.at[0])
    own_gain = pltpu.make_async_copy(gain, gainv, small_sems.at[1])
    own_tok.start()
    own_gain.start()

    def w_copy(part, k, side):
        start, width = parts[part]
        half_of = jnp.where(side == 0, 1 - m, m)
        return pltpu.make_async_copy(
            w_in.at[:, half_of, pl.ds(start, width), pl.ds(k * k_width, k_width)],
            w_parts[part].at[k, side],
            w_sems.at[part, k, side],
        )

    def wo_copy(a):
        return pltpu.make_async_copy(
            w_out.at[:, pl.ds(a * chan, chan)], wobuf.at[a], wo_sems.at[a]
        )

    col = pl.multiple_of(m * chan, chan)
    groups = ltv.shape[0]
    first_group = pl.multiple_of((s * 2 + m) * groups, groups)
    small = [
        pltpu.make_async_copy(staps.at[:, :, pl.ds(col, chan)], stv, small_sems.at[2]),
        pltpu.make_async_copy(ltaps.at[pl.ds(first_group, groups), :], ltv, small_sems.at[3]),
        pltpu.make_async_copy(bias.at[:, pl.ds(col, chan)], biasv, small_sems.at[4]),
    ]
    for copy in small:
        copy.start()
    for piece in ORDER:
        if piece[1] < W_AHEAD:
            w_copy(*piece).start()

    def lane_sums(values):
        total = None
        for k in range(values.shape[1] // 128):
            piece = values[:, k * 128 : (k + 1) * 128]
            total = piece * piece if total is None else total + piece * piece
        return total

    own_tok.wait()
    own_gain.wait()
    values = tokv[...].astype(jnp.float32)
    gained = (values * gainv[...]).astype(jnp.bfloat16)
    for k in range(n_k):
        xg[k, s] = gained[:, k * k_width : (k + 1) * k_width]
    sq_own[...] = lane_sums(values)
    pl.semaphore_wait(barrier, n_seq)

    def gather_copies(buf, send, recv):
        return [
            pltpu.make_async_remote_copy(
                src_ref=buf.at[s], dst_ref=buf.at[s],
                send_sem=send.at[j], recv_sem=recv.at[j],
                device_id={"seq": peer(shift)}, device_id_type=mesh_ids,
            )
            for j, shift in enumerate(shifts)
        ]

    gathers = [gather_copies(xg.at[k], g1_send.at[k], g1_recv.at[k]) for k in range(n_k)]
    swap = pltpu.make_async_remote_copy(
        src_ref=sq_own, dst_ref=sq_part,
        send_sem=swap_sems.at[0], recv_sem=swap_sems.at[1],
        device_id=partner, device_id_type=mesh_ids,
    )
    for copy in gathers[0]:
        copy.start()
    swap.start()

    swap.wait()
    sq_recv[s] = sq_own[...] + sq_part[...]
    sums = gather_copies(sq_recv, sq_send, sq_get)
    for copy in gathers[1] + sums:
        copy.start()

    for copy in small:
        copy.wait()
    taps = jnp.transpose(ltv[...])[:used_taps, :]
    rows = lax.broadcasted_iota(jnp.int32, (groups, chan), 0)
    cols = lax.broadcasted_iota(jnp.int32, (groups, chan), 1)
    width = chan // groups
    pick = jnp.where(
        (cols >= rows * width) & (cols < rows * width + width), 1.0, 0.0
    ).astype(jnp.bfloat16)
    high = taps.astype(jnp.bfloat16)
    rest = taps - high.astype(jnp.float32)
    mid = rest.astype(jnp.bfloat16)
    low = (rest - mid.astype(jnp.float32)).astype(jnp.bfloat16)
    tex[...] = (
        jnp.dot(high, pick, preferred_element_type=jnp.float32)
        + jnp.dot(mid, pick, preferred_element_type=jnp.float32)
    ) + jnp.dot(low, pick, preferred_element_type=jnp.float32)
    padded[:, :8, :] = jnp.zeros((3, 8, chan), jnp.float32)
    gp[:tokens, :] = jnp.zeros((tokens, chan), jnp.float32)

    for k in range(n_k - W_AHEAD):
        for piece in ORDER:
            if piece[1] == k:
                w_copy(*piece).wait()
        for piece in ORDER:
            if piece[1] == k + W_AHEAD:
                w_copy(*piece).start()
    gathers[0][-1].wait_send()
    for gather in gathers[2:]:
        for copy in gather:
            copy.start()

    def take_tokens(k):
        span = slice(k * k_width, (k + 1) * k_width)
        for copy in gathers[k]:
            copy.wait_recv()
        for a in range(n_seq):
            xf[a * t_loc : (a + 1) * t_loc, span] = xg[k, a].astype(jnp.float32)
        xb[:, span] = xf[:, span].astype(jnp.bfloat16)

    def project(part, k, side):
        if k >= n_k - W_AHEAD:
            w_copy(part, k, side).wait()
        width = parts[part][1]
        weights = w_parts[part][k, side].reshape(3 * width, k_width)
        value = contract_last(weights, xb[:, k * k_width : (k + 1) * k_width])
        if k > 0:
            value = accs[part][side] + value
        if k < n_k - 1:
            accs[part][side] = value
            return
        target = p_owns[part] if side else p_sends[part]
        for branch in range(3):
            target[branch] = jnp.transpose(value[branch * width : (branch + 1) * width])
        if side == 0:
            for branch in range(3):
                p_copy(part, branch).start()

    def p_copy(part, branch):
        return pltpu.make_async_remote_copy(
            src_ref=p_sends[part].at[branch], dst_ref=p_recvs[part].at[branch],
            send_sem=p_send_sems.at[part, branch], recv_sem=p_recv_sems.at[part, branch],
            device_id=partner, device_id_type=mesh_ids,
        )

    def take_scales():
        for copy in sums:
            copy.wait_recv()
        for a in range(n_seq):
            scales[a * t_loc : (a + 1) * t_loc, :] = sq_recv[a]
        squares = jnp.sum(scales[...], axis=1, keepdims=True)
        scales[...] = jnp.broadcast_to(lax.rsqrt(squares / D + EPSILON), scales.shape)

    def convolve(part):
        start, width = parts[part]
        span = slice(start, start + width)
        scale_rows = scales[:, :1]
        features = []
        for branch in range(3):
            p_copy(part, branch).wait()
            padded[branch, 8 : 8 + tokens, span] = (
                p_owns[part][branch] + p_recvs[part][branch]
            ) * scale_rows
            value = None
            for i in range(short_len):
                term = stv[branch, i : i + 1, span] * padded[branch, 8 - i : 8 - i + tokens, span]
                value = term if value is None else value + term
            features.append(value)
        gated = features[1] * features[2]
        gp[tokens : 2 * tokens, span] = gated
        for row in range(0, tokens, 8):
            mixed = biasv[:, span] * gated[row : row + 8]
            for i in range(min(used_taps, row + 8)):
                mixed = mixed + tex[i : i + 1, span] * gp[tokens + row - i : tokens + row - i + 8, span]
            padded[0, 8 + row : 16 + row, span] = features[0][row : row + 8] * mixed
        ggs[part][s] = padded[0, 8 : 8 + tokens, span].astype(jnp.bfloat16)
        copies = gather_copies(ggs[part], g2_send.at[part], g2_recv.at[part])
        for copy in copies:
            copy.start()
        return copies

    def fold(part, slot):
        start, width = parts[part]
        return contract_last(ggs[part][slot], wobuf[slot, :, start : start + width])

    gathers2 = {}
    for step in STEPS:
        if step[0] == "x":
            take_tokens(step[1])
            if step[1] == 1:
                for a in range(n_seq):
                    wo_copy(a).start()
        elif step[0] == "m":
            for side in step[3]:
                project(step[1], step[2], side)
        elif step[0] == "s":
            take_scales()
        else:
            gathers2[step[1]] = convolve(step[1])

    for a in range(n_seq):
        wo_copy(a).wait()
    total = fold(0, s)
    for part in range(1, len(parts)):
        total = total + fold(part, s)
    for part in range(len(parts)):
        for copy, shift in zip(gathers2[part], shifts):
            copy.wait_recv()
            total = total + fold(part, source(shift))
    facc[...] = total

    final = pltpu.make_async_remote_copy(
        src_ref=facc, dst_ref=frecv, send_sem=f_sems.at[0], recv_sem=f_sems.at[1],
        device_id=partner, device_id_type=mesh_ids,
    )
    final.start()
    for copies in [gathers[0][:-1]] + gathers[1:] + [sums] + [gathers2[part] for part in range(len(parts))]:
        for copy in copies:
            copy.wait_send()
    final.wait()
    out[...] = (facc[...] + frecv[...]).astype(out.dtype)


def fused_device(tokens_in, norm_gain, in_proj, short_taps, long_taps, skip_bias, out_proj):
    n_seq = lax.axis_size("seq")
    t_loc, half = tokens_in.shape
    tokens = n_seq * t_loc
    chan = in_proj.shape[2] // 2
    cols = out_proj.shape[0]
    group_count, filt_len = long_taps.shape
    groups = chan * group_count // D
    used_taps = min(filt_len, tokens)
    f32, bf16 = jnp.float32, jnp.bfloat16
    vmem, dma = pltpu.VMEM, pltpu.SemaphoreType.DMA
    anywhere = pl.BlockSpec(memory_space=pl.ANY)
    n_k = N_K
    k_width = half // n_k
    parts = tuple((start * chan // 512, width * chan // 512) for start, width in PARTS)
    n_p = len(parts)
    return pl.pallas_call(
        functools.partial(mixer_kernel, parts),
        name="mixer",
        out_shape=vmem((tokens, cols), bf16),
        in_specs=[anywhere] * 7,
        out_specs=pl.BlockSpec(memory_space=pltpu.VMEM),
        scratch_shapes=[
            [vmem((n_k, 2, 3, width, k_width), bf16) for _, width in parts],
            vmem((n_seq, cols, chan), bf16),
            vmem((t_loc, half), bf16),
            vmem((n_k, n_seq, t_loc, k_width), bf16),
            vmem((tokens, half), f32),
            vmem((tokens, half), bf16),
            vmem((1, half), f32),
            vmem((3, short_taps.shape[0], chan), f32),
            vmem((groups, filt_len), f32),
            vmem((1, chan), f32),
            vmem((t_loc, 128), f32),
            vmem((t_loc, 128), f32),
            vmem((n_seq, t_loc, 128), f32),
            vmem((tokens, 128), f32),
            [vmem((2, 3 * width, tokens), f32) for _, width in parts],
            [vmem((3, tokens, width), f32) for _, width in parts],
            [vmem((3, tokens, width), f32) for _, width in parts],
            [vmem((3, tokens, width), f32) for _, width in parts],
            vmem((3, 8 + tokens, chan), f32),
            vmem((2 * tokens, chan), f32),
            vmem((used_taps, chan), f32),
            [vmem((n_seq, tokens, width), bf16) for _, width in parts],
            vmem((tokens, cols), f32),
            vmem((tokens, cols), f32),
            dma((n_p, n_k, 2)),
            dma((n_seq,)),
            dma((5,)),
            dma((2,)),
            dma((n_seq - 1,)),
            dma((n_seq - 1,)),
            dma((n_p, 3)),
            dma((n_p, 3)),
            dma((n_k, n_seq - 1)),
            dma((n_k, n_seq - 1)),
            dma((n_p, n_seq - 1)),
            dma((n_p, n_seq - 1)),
            dma((2,)),
        ],
        compiler_params=pltpu.CompilerParams(
            collective_id=0, has_side_effects=True, vmem_limit_bytes=60 * 1024 * 1024
        ),
    )(
        tokens_in,
        norm_gain.reshape(1, half),
        in_proj.reshape(3, 2, chan, half),
        jnp.transpose(short_taps, (1, 0, 2)),
        long_taps,
        skip_bias.reshape(1, -1),
        out_proj.reshape(cols, -1),
    )


def fits_kernel(mesh, tokens_in, norm_gain, in_proj, short_taps, long_taps, skip_bias, out_proj):
    n_seq = mesh.shape["seq"]
    tokens = tokens_in.shape[0] // mesh.shape["grp"]
    chan = in_proj.shape[2] // 2
    half = tokens_in.shape[1] // 2
    weight_bytes = 2 * (in_proj.size + out_proj.size) // (2 * n_seq)
    return (
        n_seq == 2 * N_Z
        and mesh.shape["mdl"] == 2
        and chan % 512 == 0
        and half % 256 == 0
        and tokens % 16 == 0
        and tokens <= min(64, long_taps.shape[1])
        and short_taps.shape[0] <= 8
        and long_taps.shape[1] == 128
        and (chan * long_taps.shape[0] // D) % 8 == 0
        and weight_bytes <= 40 * 1024 * 1024
    )


def solution(mesh):
    in_specs = (
        P(("grp", "seq"), "mdl"),
        P("mdl"),
        P("seq", None, None, "mdl"),
        P(None, None, "seq"),
        P(),
        P("seq"),
        P("seq", "mdl", None),
    )
    out_specs = P("grp", "seq")

    def run(*arrays):
        body = fused_device if fits_kernel(mesh, *arrays) else per_device
        return jax.shard_map(
            body, mesh=mesh, in_specs=in_specs, out_specs=out_specs, check_vma=False
        )(*arrays)

    return run
```

```python
import functools

import jax
import jax.numpy as jnp
from jax import lax
from jax.experimental import pallas as pl
from jax.experimental.pallas import tpu as pltpu
from jax.sharding import PartitionSpec as P

D = 8192


EPSILON = 1e-06

N_Z = 4

SHIFTS = ((2, 1), (1, 1), (3, 1), (2, 0), (1, 0), (3, 0), (0, 1))
N_K = 4
W_AHEAD = 2
PARTS = ((0, 256), (256, 256))
STEPS = (
    ('x', 0),
    ('m', 0, 0, (0, 1)),
    ('m', 1, 0, (0, 1)),
    ('x', 1),
    ('m', 0, 1, (0, 1)),
    ('m', 1, 1, (0, 1)),
    ('x', 2),
    ('m', 0, 2, (0, 1)),
    ('x', 3),
    ('m', 0, 3, (0, 1)),
    ('m', 1, 2, (0,)),
    ('s',),
    ('c', 0),
    ('m', 1, 3, (0,)),
    ('m', 1, 2, (1,)),
    ('m', 1, 3, (1,)),
    ('c', 1),
)
ORDER = tuple(
    (step[1], step[2], side) for step in STEPS if step[0] == "m" for side in step[3]
)


def build_toeplitz(channel_taps):
    chan_width, filt_len = channel_taps.shape
    blank = jnp.zeros((chan_width, filt_len), jnp.float32)
    framed = jnp.concatenate([blank, channel_taps, blank], axis=1)
    flipped = framed[:, ::-1]
    repeated = jnp.tile(flipped, (1, filt_len + 1))
    window = repeated[:, filt_len - 1 : filt_len - 1 + filt_len * (3 * filt_len - 1)]
    return window.reshape(chan_width, filt_len, 3 * filt_len - 1)[:, :, : 2 * filt_len]


def mix_channels(summed, short_local, bias_local, long_taps, first_channel, chan_width):
    token_count = summed.shape[0]
    taps_short = short_local.shape[0]
    padded = jnp.pad(summed, ((taps_short - 1, 0), (0, 0), (0, 0)))
    features = jnp.zeros(summed.shape, jnp.float32)
    for offset in range(taps_short):
        features = (
            features
            + short_local[offset][None, :, :]
            * padded[taps_short - 1 - offset : taps_short - 1 - offset + token_count]
        )
    gated_prod = features[:, 1, :] * features[:, 2, :]
    group_count = long_taps.shape[0]
    filt_len = long_taps.shape[1]
    group_width = D // group_count
    channel_ids = first_channel + jnp.arange(chan_width, dtype=jnp.int32)
    select_groups = (
        channel_ids[:, None] // group_width == jnp.arange(group_count, dtype=jnp.int32)[None, :]
    ).astype(jnp.float32)
    channel_taps = jnp.dot(select_groups, long_taps, precision=lax.Precision.HIGHEST)
    toeplitz = build_toeplitz(channel_taps)
    blocks = -(-token_count // filt_len)
    framed = jnp.pad(gated_prod, ((filt_len, blocks * filt_len - token_count), (0, 0))).reshape(
        blocks + 1, filt_len, chan_width
    )
    block_pairs = jnp.concatenate([framed[:-1], framed[1:]], axis=1)
    mixed_long = jnp.einsum("ctk,nkc->ntc", toeplitz, block_pairs, precision=lax.Precision.HIGHEST)
    mixed_long = mixed_long.reshape(blocks * filt_len, chan_width)[:token_count]
    mixed_long = mixed_long + bias_local[None, :] * gated_prod
    return (features[:, 0, :] * mixed_long).astype(jnp.bfloat16)


def contract_last(left, right):
    return lax.dot_general(
        left, right, (((1,), (1,)), ((), ())), preferred_element_type=jnp.float32
    )


def per_device(tokens_in, norm_gain, in_proj, short_taps, long_taps, skip_bias, out_proj):
    half_width = tokens_in.shape[1]
    chan_dev = in_proj.shape[2] // 2
    seq_index = lax.axis_index("seq")
    mdl_index = lax.axis_index("mdl")
    weights_in = in_proj.reshape(-1, half_width)
    values = tokens_in.astype(jnp.float32)
    squares = lax.psum(jnp.sum(values * values, axis=1), "mdl")
    scale_rows = lax.rsqrt(squares / D + EPSILON)
    normed = (values * scale_rows[:, None] * norm_gain[None, :]).astype(jnp.bfloat16)
    partial_value = contract_last(lax.all_gather(normed, "seq", axis=0, tiled=True), weights_in)
    token_count = partial_value.shape[0]
    partial_value = partial_value.reshape(token_count, 3, 2, chan_dev)
    summed = lax.psum_scatter(partial_value, "mdl", scatter_dimension=2, tiled=True).reshape(
        token_count, 3, chan_dev
    )
    short_local = lax.dynamic_slice_in_dim(short_taps, mdl_index * chan_dev, chan_dev, 2)
    bias_local = lax.dynamic_slice_in_dim(skip_bias, mdl_index * chan_dev, chan_dev, 0)
    own_mixed = mix_channels(
        summed,
        short_local,
        bias_local,
        long_taps,
        seq_index * 2 * chan_dev + mdl_index * chan_dev,
        chan_dev,
    )
    out_cols = out_proj.shape[0]
    out_rows = out_proj.reshape(out_cols, -1)
    folded = contract_last(lax.all_gather(own_mixed, "seq", axis=1, tiled=True), out_rows)
    return lax.psum(folded, "mdl").astype(jnp.bfloat16)


def mixer_kernel(
    parts, tok, gain, w_in, staps, ltaps, bias, w_out, out,
    w_parts, wobuf, tokv, xg, xf, xb, gainv, stv, ltv, biasv,
    sq_own, sq_part, sq_recv, scales, accs, p_sends, p_recvs, p_owns, padded, gp, tex, ggs, facc, frecv,
    w_sems, wo_sems, small_sems, swap_sems, sq_send, sq_get, p_send_sems, p_recv_sems,
    g1_send, g1_recv, g2_send, g2_recv, f_sems,
):
    n_k, n_seq, t_loc, k_width = xg.shape
    tokens = n_seq * t_loc
    chan = stv.shape[2]
    short_len = stv.shape[1]
    used_taps = tex.shape[0]
    s = lax.axis_index("seq")
    m = lax.axis_index("mdl")
    mesh_ids = pl.DeviceIdType.MESH
    partner = {"mdl": 1 - m}
    first = lax.rem(s, 2)

    shifts = tuple((step, cross) for step, cross in SHIFTS)

    def peer(shift):
        step, cross = shift
        flip = cross * (1 - 2 * first)
        return lax.rem(s + 2 * step, n_seq) + flip

    def source(shift):
        step, cross = shift
        flip = cross * (1 - 2 * first)
        return lax.rem(s + n_seq - 2 * step, n_seq) + flip

    barrier = pltpu.get_barrier_semaphore()
    for shift in shifts:
        pl.semaphore_signal(
            barrier, inc=1, device_id={"seq": peer(shift)}, device_id_type=mesh_ids
        )
    pl.semaphore_signal(barrier, inc=1, device_id=partner, device_id_type=mesh_ids)

    own_tok = pltpu.make_async_copy(tok, tokv, small_sems.at[0])
    own_gain = pltpu.make_async_copy(gain, gainv, small_sems.at[1])
    own_tok.start()
    own_gain.start()

    def w_copy(part, k, side):
        start, width = parts[part]
        half_of = jnp.where(side == 0, 1 - m, m)
        return pltpu.make_async_copy(
            w_in.at[:, half_of, pl.ds(start, width), pl.ds(k * k_width, k_width)],
            w_parts[part].at[k, side],
            w_sems.at[part, k, side],
        )

    def wo_copy(a):
        return pltpu.make_async_copy(
            w_out.at[:, pl.ds(a * chan, chan)], wobuf.at[a], wo_sems.at[a]
        )

    col = pl.multiple_of(m * chan, chan)
    groups = ltv.shape[0]
    first_group = pl.multiple_of((s * 2 + m) * groups, groups)
    small = [
        pltpu.make_async_copy(staps.at[:, :, pl.ds(col, chan)], stv, small_sems.at[2]),
        pltpu.make_async_copy(ltaps.at[pl.ds(first_group, groups), :], ltv, small_sems.at[3]),
        pltpu.make_async_copy(bias.at[:, pl.ds(col, chan)], biasv, small_sems.at[4]),
    ]
    for copy in small:
        copy.start()
    for piece in ORDER:
        if piece[1] < W_AHEAD:
            w_copy(*piece).start()

    def lane_sums(values):
        total = None
        for k in range(values.shape[1] // 128):
            piece = values[:, k * 128 : (k + 1) * 128]
            total = piece * piece if total is None else total + piece * piece
        return total

    own_tok.wait()
    own_gain.wait()
    values = tokv[...].astype(jnp.float32)
    gained = (values * gainv[...]).astype(jnp.bfloat16)
    for k in range(n_k):
        xg[k, s] = gained[:, k * k_width : (k + 1) * k_width]
    sq_own[...] = lane_sums(values)
    pl.semaphore_wait(barrier, n_seq)

    def gather_copies(buf, send, recv):
        return [
            pltpu.make_async_remote_copy(
                src_ref=buf.at[s], dst_ref=buf.at[s],
                send_sem=send.at[j], recv_sem=recv.at[j],
                device_id={"seq": peer(shift)}, device_id_type=mesh_ids,
            )
            for j, shift in enumerate(shifts)
        ]

    gathers = [gather_copies(xg.at[k], g1_send.at[k], g1_recv.at[k]) for k in range(n_k)]
    swap = pltpu.make_async_remote_copy(
        src_ref=sq_own, dst_ref=sq_part,
        send_sem=swap_sems.at[0], recv_sem=swap_sems.at[1],
        device_id=partner, device_id_type=mesh_ids,
    )
    for copy in gathers[0]:
        copy.start()
    swap.start()

    swap.wait()
    sq_recv[s] = sq_own[...] + sq_part[...]
    sums = gather_copies(sq_recv, sq_send, sq_get)
    for copy in gathers[1] + sums:
        copy.start()

    for copy in small:
        copy.wait()
    taps = jnp.transpose(ltv[...])[:used_taps, :]
    rows = lax.broadcasted_iota(jnp.int32, (groups, chan), 0)
    cols = lax.broadcasted_iota(jnp.int32, (groups, chan), 1)
    width = chan // groups
    pick = jnp.where(
        (cols >= rows * width) & (cols < rows * width + width), 1.0, 0.0
    ).astype(jnp.bfloat16)
    high = taps.astype(jnp.bfloat16)
    rest = taps - high.astype(jnp.float32)
    mid = rest.astype(jnp.bfloat16)
    low = (rest - mid.astype(jnp.float32)).astype(jnp.bfloat16)
    tex[...] = (
        jnp.dot(high, pick, preferred_element_type=jnp.float32)
        + jnp.dot(mid, pick, preferred_element_type=jnp.float32)
    ) + jnp.dot(low, pick, preferred_element_type=jnp.float32)
    padded[:, :8, :] = jnp.zeros((3, 8, chan), jnp.float32)
    gp[:tokens, :] = jnp.zeros((tokens, chan), jnp.float32)

    for k in range(n_k - W_AHEAD):
        for piece in ORDER:
            if piece[1] == k:
                w_copy(*piece).wait()
        for piece in ORDER:
            if piece[1] == k + W_AHEAD:
                w_copy(*piece).start()
    gathers[0][-1].wait_send()
    for copy in gathers[2]:
        copy.start()

    def take_tokens(k):
        span = slice(k * k_width, (k + 1) * k_width)
        for copy in gathers[k]:
            copy.wait_recv()
        if k == 0:
            for copy in gathers[3]:
                copy.start()
        for a in range(n_seq):
            xf[a * t_loc : (a + 1) * t_loc, span] = xg[k, a].astype(jnp.float32)
        xb[:, span] = xf[:, span].astype(jnp.bfloat16)

    def project(part, k, side):
        if k >= n_k - W_AHEAD:
            w_copy(part, k, side).wait()
        width = parts[part][1]
        weights = w_parts[part][k, side].reshape(3 * width, k_width)
        value = contract_last(weights, xb[:, k * k_width : (k + 1) * k_width])
        if k > 0:
            value = accs[part][side] + value
        if k < n_k - 1:
            accs[part][side] = value
            return
        target = p_owns[part] if side else p_sends[part]
        for branch in range(3):
            target[branch] = jnp.transpose(value[branch * width : (branch + 1) * width])
        if side == 0:
            for branch in range(3):
                p_copy(part, branch).start()

    def p_copy(part, branch):
        return pltpu.make_async_remote_copy(
            src_ref=p_sends[part].at[branch], dst_ref=p_recvs[part].at[branch],
            send_sem=p_send_sems.at[part, branch], recv_sem=p_recv_sems.at[part, branch],
            device_id=partner, device_id_type=mesh_ids,
        )

    def take_scales():
        for copy in sums:
            copy.wait_recv()
        for a in range(n_seq):
            scales[a * t_loc : (a + 1) * t_loc, :] = sq_recv[a]
        squares = jnp.sum(scales[...], axis=1, keepdims=True)
        scales[...] = jnp.broadcast_to(lax.rsqrt(squares / D + EPSILON), scales.shape)

    def convolve(part):
        start, width = parts[part]
        span = slice(start, start + width)
        scale_rows = scales[:, :1]
        features = []
        for branch in range(3):
            p_copy(part, branch).wait()
            padded[branch, 8 : 8 + tokens, span] = (
                p_owns[part][branch] + p_recvs[part][branch]
            ) * scale_rows
            value = None
            for i in range(short_len):
                term = stv[branch, i : i + 1, span] * padded[branch, 8 - i : 8 - i + tokens, span]
                value = term if value is None else value + term
            features.append(value)
        gated = features[1] * features[2]
        gp[tokens : 2 * tokens, span] = gated
        for row in range(0, tokens, 8):
            mixed = biasv[:, span] * gated[row : row + 8]
            for i in range(min(used_taps, row + 8)):
                mixed = mixed + tex[i : i + 1, span] * gp[tokens + row - i : tokens + row - i + 8, span]
            padded[0, 8 + row : 16 + row, span] = features[0][row : row + 8] * mixed
        ggs[part][s] = padded[0, 8 : 8 + tokens, span].astype(jnp.bfloat16)
        copies = gather_copies(ggs[part], g2_send.at[part], g2_recv.at[part])
        for copy in copies:
            copy.start()
        return copies

    def fold(part, slot):
        start, width = parts[part]
        return contract_last(ggs[part][slot], wobuf[slot, :, start : start + width])

    gathers2 = {}
    for step in STEPS:
        if step[0] == "x":
            take_tokens(step[1])
            if step[1] == 1:
                for a in range(n_seq):
                    wo_copy(a).start()
        elif step[0] == "m":
            for side in step[3]:
                project(step[1], step[2], side)
        elif step[0] == "s":
            take_scales()
        else:
            gathers2[step[1]] = convolve(step[1])

    for a in range(n_seq):
        wo_copy(a).wait()
    total = fold(0, s)
    for part in range(1, len(parts)):
        total = total + fold(part, s)
    for part in range(len(parts)):
        for copy, shift in zip(gathers2[part], shifts):
            copy.wait_recv()
            total = total + fold(part, source(shift))
    facc[...] = total

    final = pltpu.make_async_remote_copy(
        src_ref=facc, dst_ref=frecv, send_sem=f_sems.at[0], recv_sem=f_sems.at[1],
        device_id=partner, device_id_type=mesh_ids,
    )
    final.start()
    for copies in [gathers[0][:-1]] + gathers[1:] + [sums] + [gathers2[part] for part in range(len(parts))]:
        for copy in copies:
            copy.wait_send()
    final.wait()
    out[...] = (facc[...] + frecv[...]).astype(out.dtype)


def fused_device(tokens_in, norm_gain, in_proj, short_taps, long_taps, skip_bias, out_proj):
    n_seq = lax.axis_size("seq")
    t_loc, half = tokens_in.shape
    tokens = n_seq * t_loc
    chan = in_proj.shape[2] // 2
    cols = out_proj.shape[0]
    group_count, filt_len = long_taps.shape
    groups = chan * group_count // D
    used_taps = min(filt_len, tokens)
    f32, bf16 = jnp.float32, jnp.bfloat16
    vmem, dma = pltpu.VMEM, pltpu.SemaphoreType.DMA
    anywhere = pl.BlockSpec(memory_space=pl.ANY)
    n_k = N_K
    k_width = half // n_k
    parts = tuple((start * chan // 512, width * chan // 512) for start, width in PARTS)
    n_p = len(parts)
    return pl.pallas_call(
        functools.partial(mixer_kernel, parts),
        name="mixer",
        out_shape=vmem((tokens, cols), bf16),
        in_specs=[anywhere] * 7,
        out_specs=pl.BlockSpec(memory_space=pltpu.VMEM),
        scratch_shapes=[
            [vmem((n_k, 2, 3, width, k_width), bf16) for _, width in parts],
            vmem((n_seq, cols, chan), bf16),
            vmem((t_loc, half), bf16),
            vmem((n_k, n_seq, t_loc, k_width), bf16),
            vmem((tokens, half), f32),
            vmem((tokens, half), bf16),
            vmem((1, half), f32),
            vmem((3, short_taps.shape[0], chan), f32),
            vmem((groups, filt_len), f32),
            vmem((1, chan), f32),
            vmem((t_loc, 128), f32),
            vmem((t_loc, 128), f32),
            vmem((n_seq, t_loc, 128), f32),
            vmem((tokens, 128), f32),
            [vmem((2, 3 * width, tokens), f32) for _, width in parts],
            [vmem((3, tokens, width), f32) for _, width in parts],
            [vmem((3, tokens, width), f32) for _, width in parts],
            [vmem((3, tokens, width), f32) for _, width in parts],
            vmem((3, 8 + tokens, chan), f32),
            vmem((2 * tokens, chan), f32),
            vmem((used_taps, chan), f32),
            [vmem((n_seq, tokens, width), bf16) for _, width in parts],
            vmem((tokens, cols), f32),
            vmem((tokens, cols), f32),
            dma((n_p, n_k, 2)),
            dma((n_seq,)),
            dma((5,)),
            dma((2,)),
            dma((n_seq - 1,)),
            dma((n_seq - 1,)),
            dma((n_p, 3)),
            dma((n_p, 3)),
            dma((n_k, n_seq - 1)),
            dma((n_k, n_seq - 1)),
            dma((n_p, n_seq - 1)),
            dma((n_p, n_seq - 1)),
            dma((2,)),
        ],
        compiler_params=pltpu.CompilerParams(
            collective_id=0, has_side_effects=True, vmem_limit_bytes=60 * 1024 * 1024
        ),
    )(
        tokens_in,
        norm_gain.reshape(1, half),
        in_proj.reshape(3, 2, chan, half),
        jnp.transpose(short_taps, (1, 0, 2)),
        long_taps,
        skip_bias.reshape(1, -1),
        out_proj.reshape(cols, -1),
    )


def fits_kernel(mesh, tokens_in, norm_gain, in_proj, short_taps, long_taps, skip_bias, out_proj):
    n_seq = mesh.shape["seq"]
    tokens = tokens_in.shape[0] // mesh.shape["grp"]
    chan = in_proj.shape[2] // 2
    half = tokens_in.shape[1] // 2
    weight_bytes = 2 * (in_proj.size + out_proj.size) // (2 * n_seq)
    return (
        n_seq == 2 * N_Z
        and mesh.shape["mdl"] == 2
        and chan % 512 == 0
        and half % 256 == 0
        and tokens % 16 == 0
        and tokens <= min(64, long_taps.shape[1])
        and short_taps.shape[0] <= 8
        and long_taps.shape[1] == 128
        and (chan * long_taps.shape[0] // D) % 8 == 0
        and weight_bytes <= 40 * 1024 * 1024
    )


def solution(mesh):
    in_specs = (
        P(("grp", "seq"), "mdl"),
        P("mdl"),
        P("seq", None, None, "mdl"),
        P(None, None, "seq"),
        P(),
        P("seq"),
        P("seq", "mdl", None),
    )
    out_specs = P("grp", "seq")

    def run(*arrays):
        body = fused_device if fits_kernel(mesh, *arrays) else per_device
        return jax.shard_map(
            body, mesh=mesh, in_specs=in_specs, out_specs=out_specs, check_vma=False
        )(*arrays)

    return run
```

```python
import functools

import jax
import jax.numpy as jnp
from jax import lax
from jax.experimental import pallas as pl
from jax.experimental.pallas import tpu as pltpu
from jax.sharding import PartitionSpec as P

D = 8192


EPSILON = 1e-06

N_Z = 4

SHIFTS = ((2, 1), (1, 1), (3, 1), (2, 0), (1, 0), (3, 0), (0, 1))
N_K = 4
W_AHEAD = 2
PARTS = ((0, 256), (256, 256))
STEPS = (
    ('x', 0),
    ('m', 0, 0, (0, 1)),
    ('m', 1, 0, (0, 1)),
    ('x', 1),
    ('m', 0, 1, (0, 1)),
    ('m', 1, 1, (0, 1)),
    ('x', 2),
    ('m', 0, 2, (0,)),
    ('x', 3),
    ('m', 0, 3, (0,)),
    ('m', 0, 2, (1,)),
    ('m', 0, 3, (1,)),
    ('s',),
    ('c', 0),
    ('m', 1, 2, (0,)),
    ('m', 1, 3, (0,)),
    ('m', 1, 2, (1,)),
    ('m', 1, 3, (1,)),
    ('c', 1),
)
ORDER = tuple(
    (step[1], step[2], side) for step in STEPS if step[0] == "m" for side in step[3]
)


def build_toeplitz(channel_taps):
    chan_width, filt_len = channel_taps.shape
    blank = jnp.zeros((chan_width, filt_len), jnp.float32)
    framed = jnp.concatenate([blank, channel_taps, blank], axis=1)
    flipped = framed[:, ::-1]
    repeated = jnp.tile(flipped, (1, filt_len + 1))
    window = repeated[:, filt_len - 1 : filt_len - 1 + filt_len * (3 * filt_len - 1)]
    return window.reshape(chan_width, filt_len, 3 * filt_len - 1)[:, :, : 2 * filt_len]


def mix_channels(summed, short_local, bias_local, long_taps, first_channel, chan_width):
    token_count = summed.shape[0]
    taps_short = short_local.shape[0]
    padded = jnp.pad(summed, ((taps_short - 1, 0), (0, 0), (0, 0)))
    features = jnp.zeros(summed.shape, jnp.float32)
    for offset in range(taps_short):
        features = (
            features
            + short_local[offset][None, :, :]
            * padded[taps_short - 1 - offset : taps_short - 1 - offset + token_count]
        )
    gated_prod = features[:, 1, :] * features[:, 2, :]
    group_count = long_taps.shape[0]
    filt_len = long_taps.shape[1]
    group_width = D // group_count
    channel_ids = first_channel + jnp.arange(chan_width, dtype=jnp.int32)
    select_groups = (
        channel_ids[:, None] // group_width == jnp.arange(group_count, dtype=jnp.int32)[None, :]
    ).astype(jnp.float32)
    channel_taps = jnp.dot(select_groups, long_taps, precision=lax.Precision.HIGHEST)
    toeplitz = build_toeplitz(channel_taps)
    blocks = -(-token_count // filt_len)
    framed = jnp.pad(gated_prod, ((filt_len, blocks * filt_len - token_count), (0, 0))).reshape(
        blocks + 1, filt_len, chan_width
    )
    block_pairs = jnp.concatenate([framed[:-1], framed[1:]], axis=1)
    mixed_long = jnp.einsum("ctk,nkc->ntc", toeplitz, block_pairs, precision=lax.Precision.HIGHEST)
    mixed_long = mixed_long.reshape(blocks * filt_len, chan_width)[:token_count]
    mixed_long = mixed_long + bias_local[None, :] * gated_prod
    return (features[:, 0, :] * mixed_long).astype(jnp.bfloat16)


def contract_last(left, right):
    return lax.dot_general(
        left, right, (((1,), (1,)), ((), ())), preferred_element_type=jnp.float32
    )


def per_device(tokens_in, norm_gain, in_proj, short_taps, long_taps, skip_bias, out_proj):
    half_width = tokens_in.shape[1]
    chan_dev = in_proj.shape[2] // 2
    seq_index = lax.axis_index("seq")
    mdl_index = lax.axis_index("mdl")
    weights_in = in_proj.reshape(-1, half_width)
    values = tokens_in.astype(jnp.float32)
    squares = lax.psum(jnp.sum(values * values, axis=1), "mdl")
    scale_rows = lax.rsqrt(squares / D + EPSILON)
    normed = (values * scale_rows[:, None] * norm_gain[None, :]).astype(jnp.bfloat16)
    partial_value = contract_last(lax.all_gather(normed, "seq", axis=0, tiled=True), weights_in)
    token_count = partial_value.shape[0]
    partial_value = partial_value.reshape(token_count, 3, 2, chan_dev)
    summed = lax.psum_scatter(partial_value, "mdl", scatter_dimension=2, tiled=True).reshape(
        token_count, 3, chan_dev
    )
    short_local = lax.dynamic_slice_in_dim(short_taps, mdl_index * chan_dev, chan_dev, 2)
    bias_local = lax.dynamic_slice_in_dim(skip_bias, mdl_index * chan_dev, chan_dev, 0)
    own_mixed = mix_channels(
        summed,
        short_local,
        bias_local,
        long_taps,
        seq_index * 2 * chan_dev + mdl_index * chan_dev,
        chan_dev,
    )
    out_cols = out_proj.shape[0]
    out_rows = out_proj.reshape(out_cols, -1)
    folded = contract_last(lax.all_gather(own_mixed, "seq", axis=1, tiled=True), out_rows)
    return lax.psum(folded, "mdl").astype(jnp.bfloat16)


def mixer_kernel(
    parts, tok, gain, w_in, staps, ltaps, bias, w_out, out,
    w_parts, wobuf, tokv, xg, xf, xb, gainv, stv, ltv, biasv,
    sq_own, sq_part, sq_recv, scales, accs, p_sends, p_recvs, p_owns, padded, gp, tex, ggs, facc, frecv,
    w_sems, wo_sems, small_sems, swap_sems, sq_send, sq_get, p_send_sems, p_recv_sems,
    g1_send, g1_recv, g2_send, g2_recv, f_sems,
):
    n_k, n_seq, t_loc, k_width = xg.shape
    tokens = n_seq * t_loc
    chan = stv.shape[2]
    short_len = stv.shape[1]
    used_taps = tex.shape[0]
    s = lax.axis_index("seq")
    m = lax.axis_index("mdl")
    mesh_ids = pl.DeviceIdType.MESH
    partner = {"mdl": 1 - m}
    first = lax.rem(s, 2)

    shifts = tuple((step, cross) for step, cross in SHIFTS)

    def peer(shift):
        step, cross = shift
        flip = cross * (1 - 2 * first)
        return lax.rem(s + 2 * step, n_seq) + flip

    def source(shift):
        step, cross = shift
        flip = cross * (1 - 2 * first)
        return lax.rem(s + n_seq - 2 * step, n_seq) + flip

    barrier = pltpu.get_barrier_semaphore()
    for shift in shifts:
        pl.semaphore_signal(
            barrier, inc=1, device_id={"seq": peer(shift)}, device_id_type=mesh_ids
        )
    pl.semaphore_signal(barrier, inc=1, device_id=partner, device_id_type=mesh_ids)

    own_tok = pltpu.make_async_copy(tok, tokv, small_sems.at[0])
    own_gain = pltpu.make_async_copy(gain, gainv, small_sems.at[1])
    own_tok.start()
    own_gain.start()

    def w_copy(part, k, side):
        start, width = parts[part]
        half_of = jnp.where(side == 0, 1 - m, m)
        return pltpu.make_async_copy(
            w_in.at[:, half_of, pl.ds(start, width), pl.ds(k * k_width, k_width)],
            w_parts[part].at[k, side],
            w_sems.at[part, k, side],
        )

    def wo_copy(a):
        return pltpu.make_async_copy(
            w_out.at[:, pl.ds(a * chan, chan)], wobuf.at[a], wo_sems.at[a]
        )

    col = pl.multiple_of(m * chan, chan)
    groups = ltv.shape[0]
    first_group = pl.multiple_of((s * 2 + m) * groups, groups)
    small = [
        pltpu.make_async_copy(staps.at[:, :, pl.ds(col, chan)], stv, small_sems.at[2]),
        pltpu.make_async_copy(ltaps.at[pl.ds(first_group, groups), :], ltv, small_sems.at[3]),
        pltpu.make_async_copy(bias.at[:, pl.ds(col, chan)], biasv, small_sems.at[4]),
    ]
    for copy in small:
        copy.start()
    for piece in ORDER:
        if piece[1] < W_AHEAD:
            w_copy(*piece).start()

    def lane_sums(values):
        total = None
        for k in range(values.shape[1] // 128):
            piece = values[:, k * 128 : (k + 1) * 128]
            total = piece * piece if total is None else total + piece * piece
        return total

    own_tok.wait()
    own_gain.wait()
    values = tokv[...].astype(jnp.float32)
    gained = (values * gainv[...]).astype(jnp.bfloat16)
    for k in range(n_k):
        xg[k, s] = gained[:, k * k_width : (k + 1) * k_width]
    sq_own[...] = lane_sums(values)
    pl.semaphore_wait(barrier, n_seq)

    def gather_copies(buf, send, recv):
        return [
            pltpu.make_async_remote_copy(
                src_ref=buf.at[s], dst_ref=buf.at[s],
                send_sem=send.at[j], recv_sem=recv.at[j],
                device_id={"seq": peer(shift)}, device_id_type=mesh_ids,
            )
            for j, shift in enumerate(shifts)
        ]

    gathers = [gather_copies(xg.at[k], g1_send.at[k], g1_recv.at[k]) for k in range(n_k)]
    swap = pltpu.make_async_remote_copy(
        src_ref=sq_own, dst_ref=sq_part,
        send_sem=swap_sems.at[0], recv_sem=swap_sems.at[1],
        device_id=partner, device_id_type=mesh_ids,
    )
    for copy in gathers[0]:
        copy.start()
    swap.start()

    swap.wait()
    sq_recv[s] = sq_own[...] + sq_part[...]
    sums = gather_copies(sq_recv, sq_send, sq_get)
    for copy in gathers[1] + sums:
        copy.start()

    for copy in small:
        copy.wait()
    taps = jnp.transpose(ltv[...])[:used_taps, :]
    rows = lax.broadcasted_iota(jnp.int32, (groups, chan), 0)
    cols = lax.broadcasted_iota(jnp.int32, (groups, chan), 1)
    width = chan // groups
    pick = jnp.where(
        (cols >= rows * width) & (cols < rows * width + width), 1.0, 0.0
    ).astype(jnp.bfloat16)
    high = taps.astype(jnp.bfloat16)
    rest = taps - high.astype(jnp.float32)
    mid = rest.astype(jnp.bfloat16)
    low = (rest - mid.astype(jnp.float32)).astype(jnp.bfloat16)
    tex[...] = (
        jnp.dot(high, pick, preferred_element_type=jnp.float32)
        + jnp.dot(mid, pick, preferred_element_type=jnp.float32)
    ) + jnp.dot(low, pick, preferred_element_type=jnp.float32)
    padded[:, :8, :] = jnp.zeros((3, 8, chan), jnp.float32)
    gp[:tokens, :] = jnp.zeros((tokens, chan), jnp.float32)

    for k in range(n_k - W_AHEAD):
        for piece in ORDER:
            if piece[1] == k:
                w_copy(*piece).wait()
        for piece in ORDER:
            if piece[1] == k + W_AHEAD:
                w_copy(*piece).start()
    gathers[0][-1].wait_send()
    for copy in gathers[2]:
        copy.start()

    def take_tokens(k):
        span = slice(k * k_width, (k + 1) * k_width)
        for copy in gathers[k]:
            copy.wait_recv()
        if k == 0:
            for copy in gathers[3]:
                copy.start()
        for a in range(n_seq):
            xf[a * t_loc : (a + 1) * t_loc, span] = xg[k, a].astype(jnp.float32)
        xb[:, span] = xf[:, span].astype(jnp.bfloat16)

    def project(part, k, side):
        if k >= n_k - W_AHEAD:
            w_copy(part, k, side).wait()
        width = parts[part][1]
        weights = w_parts[part][k, side].reshape(3 * width, k_width)
        value = contract_last(weights, xb[:, k * k_width : (k + 1) * k_width])
        if k > 0:
            value = accs[part][side] + value
        if k < n_k - 1:
            accs[part][side] = value
            return
        target = p_owns[part] if side else p_sends[part]
        for branch in range(3):
            target[branch] = jnp.transpose(value[branch * width : (branch + 1) * width])
        if side == 0:
            for branch in range(3):
                p_copy(part, branch).start()

    def p_copy(part, branch):
        return pltpu.make_async_remote_copy(
            src_ref=p_sends[part].at[branch], dst_ref=p_recvs[part].at[branch],
            send_sem=p_send_sems.at[part, branch], recv_sem=p_recv_sems.at[part, branch],
            device_id=partner, device_id_type=mesh_ids,
        )

    def take_scales():
        for copy in sums:
            copy.wait_recv()
        for a in range(n_seq):
            scales[a * t_loc : (a + 1) * t_loc, :] = sq_recv[a]
        squares = jnp.sum(scales[...], axis=1, keepdims=True)
        scales[...] = jnp.broadcast_to(lax.rsqrt(squares / D + EPSILON), scales.shape)

    def convolve(part):
        start, width = parts[part]
        span = slice(start, start + width)
        scale_rows = scales[:, :1]
        features = []
        for branch in range(3):
            p_copy(part, branch).wait()
            padded[branch, 8 : 8 + tokens, span] = (
                p_owns[part][branch] + p_recvs[part][branch]
            ) * scale_rows
            value = None
            for i in range(short_len):
                term = stv[branch, i : i + 1, span] * padded[branch, 8 - i : 8 - i + tokens, span]
                value = term if value is None else value + term
            features.append(value)
        gated = features[1] * features[2]
        gp[tokens : 2 * tokens, span] = gated
        for row in range(0, tokens, 8):
            mixed = biasv[:, span] * gated[row : row + 8]
            for i in range(min(used_taps, row + 8)):
                mixed = mixed + tex[i : i + 1, span] * gp[tokens + row - i : tokens + row - i + 8, span]
            padded[0, 8 + row : 16 + row, span] = features[0][row : row + 8] * mixed
        ggs[part][s] = padded[0, 8 : 8 + tokens, span].astype(jnp.bfloat16)
        copies = gather_copies(ggs[part], g2_send.at[part], g2_recv.at[part])
        for copy in copies:
            copy.start()
        return copies

    def fold(part, slot):
        start, width = parts[part]
        return contract_last(ggs[part][slot], wobuf[slot, :, start : start + width])

    gathers2 = {}
    for step in STEPS:
        if step[0] == "x":
            take_tokens(step[1])
            if step[1] == 1:
                for a in range(n_seq):
                    wo_copy(a).start()
        elif step[0] == "m":
            for side in step[3]:
                project(step[1], step[2], side)
        elif step[0] == "s":
            take_scales()
        else:
            gathers2[step[1]] = convolve(step[1])

    for a in range(n_seq):
        wo_copy(a).wait()
    total = fold(0, s)
    for part in range(1, len(parts)):
        total = total + fold(part, s)
    for part in range(len(parts)):
        for copy, shift in zip(gathers2[part], shifts):
            copy.wait_recv()
            total = total + fold(part, source(shift))
    facc[...] = total

    final = pltpu.make_async_remote_copy(
        src_ref=facc, dst_ref=frecv, send_sem=f_sems.at[0], recv_sem=f_sems.at[1],
        device_id=partner, device_id_type=mesh_ids,
    )
    final.start()
    for copies in [gathers[0][:-1]] + gathers[1:] + [sums] + [gathers2[part] for part in range(len(parts))]:
        for copy in copies:
            copy.wait_send()
    final.wait()
    out[...] = (facc[...] + frecv[...]).astype(out.dtype)


def fused_device(tokens_in, norm_gain, in_proj, short_taps, long_taps, skip_bias, out_proj):
    n_seq = lax.axis_size("seq")
    t_loc, half = tokens_in.shape
    tokens = n_seq * t_loc
    chan = in_proj.shape[2] // 2
    cols = out_proj.shape[0]
    group_count, filt_len = long_taps.shape
    groups = chan * group_count // D
    used_taps = min(filt_len, tokens)
    f32, bf16 = jnp.float32, jnp.bfloat16
    vmem, dma = pltpu.VMEM, pltpu.SemaphoreType.DMA
    anywhere = pl.BlockSpec(memory_space=pl.ANY)
    n_k = N_K
    k_width = half // n_k
    parts = tuple((start * chan // 512, width * chan // 512) for start, width in PARTS)
    n_p = len(parts)
    return pl.pallas_call(
        functools.partial(mixer_kernel, parts),
        name="mixer",
        out_shape=vmem((tokens, cols), bf16),
        in_specs=[anywhere] * 7,
        out_specs=pl.BlockSpec(memory_space=pltpu.VMEM),
        scratch_shapes=[
            [vmem((n_k, 2, 3, width, k_width), bf16) for _, width in parts],
            vmem((n_seq, cols, chan), bf16),
            vmem((t_loc, half), bf16),
            vmem((n_k, n_seq, t_loc, k_width), bf16),
            vmem((tokens, half), f32),
            vmem((tokens, half), bf16),
            vmem((1, half), f32),
            vmem((3, short_taps.shape[0], chan), f32),
            vmem((groups, filt_len), f32),
            vmem((1, chan), f32),
            vmem((t_loc, 128), f32),
            vmem((t_loc, 128), f32),
            vmem((n_seq, t_loc, 128), f32),
            vmem((tokens, 128), f32),
            [vmem((2, 3 * width, tokens), f32) for _, width in parts],
            [vmem((3, tokens, width), f32) for _, width in parts],
            [vmem((3, tokens, width), f32) for _, width in parts],
            [vmem((3, tokens, width), f32) for _, width in parts],
            vmem((3, 8 + tokens, chan), f32),
            vmem((2 * tokens, chan), f32),
            vmem((used_taps, chan), f32),
            [vmem((n_seq, tokens, width), bf16) for _, width in parts],
            vmem((tokens, cols), f32),
            vmem((tokens, cols), f32),
            dma((n_p, n_k, 2)),
            dma((n_seq,)),
            dma((5,)),
            dma((2,)),
            dma((n_seq - 1,)),
            dma((n_seq - 1,)),
            dma((n_p, 3)),
            dma((n_p, 3)),
            dma((n_k, n_seq - 1)),
            dma((n_k, n_seq - 1)),
            dma((n_p, n_seq - 1)),
            dma((n_p, n_seq - 1)),
            dma((2,)),
        ],
        compiler_params=pltpu.CompilerParams(
            collective_id=0, has_side_effects=True, vmem_limit_bytes=60 * 1024 * 1024
        ),
    )(
        tokens_in,
        norm_gain.reshape(1, half),
        in_proj.reshape(3, 2, chan, half),
        jnp.transpose(short_taps, (1, 0, 2)),
        long_taps,
        skip_bias.reshape(1, -1),
        out_proj.reshape(cols, -1),
    )


def fits_kernel(mesh, tokens_in, norm_gain, in_proj, short_taps, long_taps, skip_bias, out_proj):
    n_seq = mesh.shape["seq"]
    tokens = tokens_in.shape[0] // mesh.shape["grp"]
    chan = in_proj.shape[2] // 2
    half = tokens_in.shape[1] // 2
    weight_bytes = 2 * (in_proj.size + out_proj.size) // (2 * n_seq)
    return (
        n_seq == 2 * N_Z
        and mesh.shape["mdl"] == 2
        and chan % 512 == 0
        and half % 256 == 0
        and tokens % 16 == 0
        and tokens <= min(64, long_taps.shape[1])
        and short_taps.shape[0] <= 8
        and long_taps.shape[1] == 128
        and (chan * long_taps.shape[0] // D) % 8 == 0
        and weight_bytes <= 40 * 1024 * 1024
    )


def solution(mesh):
    in_specs = (
        P(("grp", "seq"), "mdl"),
        P("mdl"),
        P("seq", None, None, "mdl"),
        P(None, None, "seq"),
        P(),
        P("seq"),
        P("seq", "mdl", None),
    )
    out_specs = P("grp", "seq")

    def run(*arrays):
        body = fused_device if fits_kernel(mesh, *arrays) else per_device
        return jax.shard_map(
            body, mesh=mesh, in_specs=in_specs, out_specs=out_specs, check_vma=False
        )(*arrays)

    return run
```
